128 devices in a mesh: tm: 4 (over y_hi, core), stn: 32 (over z, x, y_lo).
Axes of the slice: x: 4, y: 4 (y_hi: 2, y_lo: 2; y = y_hi * 2 + y_lo), z: 4, core: 2. Of those that a mesh axis runs over, the one named last changes fastest.
Arguments:
- voltages: bfloat16 [1024, 524288], P('stn', 'tm'), may hold values from -6 to 6
- delays: int32 [1024], P('stn'), may hold values from 0 to 511
- phases: int32 [1024], P('stn'), may hold values from 0 to 32767
- flags: int32 [1024], P('stn'), may hold values 0 or 1
Outputs:
- visibility: float32 [512, 1024, 1024], P(('tm', 'stn'))
The draws below stay inside these ranges and needn't reach their ends.
All inputs are finite; a program needn't handle non-finite values. No bound on the sum of `flags` on one device may be relied on, other than what follows from the above.
Results may differ from the reference program's by a relative error of at most 0.0038.
Values may be sent and summed in bfloat16 or wider, within the bound.
No kernel may reach another device: no remote copies, remote signals or barrier semaphores. Data moves between devices by JAX's collectives and lax.ppermute only.
A program may use at most 192 MiB of HBM per device.

```python
import math
import jax
import jax.numpy as jnp
from jax import lax

STN_DEV = 32
NFFT = 512
TAPS = 4
NFINE = 64
AVG = 4
STREAMS = 1024
SPECTRA = 16
SAMPLES = 524288
BANDS = 32
GROUPS = 512


def touch_ends(array, stream_key, smallest, high):
    shape = array.shape
    place = [jax.random.randint(jax.random.fold_in(stream_key, axis), (), 0, shape[axis]) for axis in range(len(shape))]
    array = array.at[tuple(place)].set(smallest)
    longest = shape.index(max(shape))
    place[longest] = (place[longest] + 1) % shape[longest]
    return array.at[tuple(place)].set(high)


def shard_levels(stream_key, dims, pieces, low, top_value):
    def one(axis_at, shards_of):
        steps = jax.random.uniform(jax.random.fold_in(jax.random.fold_in(stream_key, 6), axis_at), (shards_of,), jnp.float32, low / len(pieces), top_value / len(pieces))
        return jnp.repeat(jnp.exp(steps), dims[axis_at] // shards_of).reshape((-1,) + (1,) * (len(dims) - axis_at - 1))

    level = one(*pieces[0])
    for cut in pieces[1:]:
        level = level * one(*cut)
    return level


def centred(own_key, extent, deviation, most, shards=(), kind=jnp.bfloat16):
    drawn = jax.random.normal(own_key, extent, jnp.float32) * deviation
    if len(shards) > 0:
        drawn = shard_levels(own_key, extent, shards, -0.22, 0.18) * drawn
    return jnp.clip(drawn, min=-most, max=most).astype(kind)


def setup_inputs(seed: int = 0) -> dict:
    streams_of = jax.random.split(jax.random.key(seed), 5)
    voltages = centred(streams_of[0], (STREAMS, SAMPLES), 1.0, 6.0, ((0, 32), (1, 4)))
    delays = touch_ends(jax.random.randint(streams_of[1], (STREAMS,), 0, NFFT), jax.random.fold_in(streams_of[1], 1), 0, NFFT - 1).astype(jnp.int32)
    phases = touch_ends(jax.random.randint(streams_of[2], (STREAMS,), 0, NFFT * NFINE), jax.random.fold_in(streams_of[2], 1), 0, (NFFT * NFINE) - 1).astype(jnp.int32)
    flags = touch_ends((jax.random.randint(streams_of[3], (STREAMS,), 0, 8) < 7).astype(jnp.int32), jax.random.fold_in(streams_of[3], 1), 0, 1)
    return dict(voltages=voltages, delays=delays, phases=phases, flags=flags)


def pfb_window():
    length = TAPS * NFFT
    places = jnp.arange(length, dtype=jnp.float32)
    offsets = (places - length / 2 + 0.5) / NFFT
    taper = 0.54 - 0.46 * jnp.cos(2.0 * math.pi * places / (length - 1))
    return (jnp.sinc(offsets) * taper).reshape(TAPS, NFFT)

def coarse_table(band_total):
    sample_ids = jnp.arange(NFFT, dtype=jnp.int32)
    channel_ids = jnp.arange(band_total, dtype=jnp.int32) + 1
    product = jnp.mod(channel_ids[:, None] * sample_ids[None, :], NFFT)
    angles = product.astype(jnp.float32) * (2.0 * math.pi / NFFT)
    factor = 1.0 / math.sqrt(NFFT)
    return jnp.stack([jnp.cos(angles) * factor, -jnp.sin(angles) * factor], 0)

def fine_table():
    frame_ids = jnp.arange(NFINE, dtype=jnp.int32)
    channel_ids = frame_ids - NFINE // 2
    product = jnp.mod(frame_ids[:, None] * channel_ids[None, :], NFINE)
    angles = product.astype(jnp.float32) * (2.0 * math.pi / NFINE)
    cosine = jnp.cos(angles) / math.sqrt(NFINE)
    sine_part = jnp.sin(angles) / math.sqrt(NFINE)
    return jnp.stack([jnp.stack([cosine, -sine_part], 1), jnp.stack([sine_part, cosine], 1)], 0)

def polyphase(volts, rim_part):
    extended = jnp.concatenate([volts, rim_part], 1).astype(jnp.float32)
    streams_here = volts.shape[0]
    count = volts.shape[1] // NFFT
    window = pfb_window()
    framed = jnp.zeros((streams_here, count, NFFT), jnp.float32)
    for tap_index in range(TAPS):
        piece = extended[:, tap_index * NFFT:tap_index * NFFT + count * NFFT]
        framed = framed + piece.reshape(streams_here, count, NFFT) * window[tap_index]
    return framed

def channelize_packed(shaped, band_ids, delay_part, phase_part, flag_part):
    per_band = NFINE // AVG
    table = fine_table().reshape(2, NFINE, 2, per_band, AVG)
    fine = jnp.einsum('rbstm,rmqga->bgsqat', shaped, table, precision=lax.Precision.HIGHEST)
    fine_ids = jnp.arange(NFINE, dtype=jnp.int32).reshape(per_band, AVG)
    freq = (band_ids[:, None, None] + 1) * NFINE + fine_ids[None] - NFINE // 2
    index = jnp.mod(delay_part[None, None, :, None] * freq[:, :, None, :] + phase_part[None, None, :, None], NFFT * NFINE)
    angles = index.astype(jnp.float32) * (-2.0 * math.pi / (NFFT * NFINE))
    cosine = jnp.cos(angles)[..., None]
    sine_part = jnp.sin(angles)[..., None]
    keep = flag_part.astype(jnp.float32)[None, None, :, None, None]
    real_part = fine[:, :, :, 0]
    imag_part = fine[:, :, :, 1]
    new_real = (real_part * cosine - imag_part * sine_part) * keep
    new_imag = (real_part * sine_part + imag_part * cosine) * keep
    packed = jnp.stack([new_real, new_imag], 3).astype(jnp.bfloat16)
    band_count, groups_here, streams_here = (packed.shape[0], packed.shape[1], packed.shape[2])
    return packed.reshape(band_count * groups_here, streams_here, 2 * AVG * packed.shape[-1])

def packed_gram(block, outer, factor):
    rows, width = block.shape
    viewed = block.reshape(rows, outer, 2, width // (2 * outer))
    swapped = jnp.concatenate([-viewed[:, :, 1:2], viewed[:, :, 0:1]], 2).reshape(rows, width)
    real_part = jnp.dot(block, block.T, preferred_element_type=jnp.float32)
    imag_part = jnp.dot(block, swapped.T, preferred_element_type=jnp.float32)
    row_ids = jnp.arange(rows, dtype=jnp.int32)
    upper = row_ids[None, :] >= row_ids[:, None]
    return jnp.where(upper, real_part, imag_part) * factor

def reference(voltages, delays, phases, flags):
    blocks = STREAMS // STN_DEV
    coarse_tab = coarse_table(BANDS)
    band_ids = jnp.arange(BANDS, dtype=jnp.int32)

    def channelize(inputs):
        volts, delay_part, phase_part, flag_part = inputs
        rim_part = jnp.zeros((STN_DEV, (TAPS - 1) * NFFT), jnp.bfloat16)
        framed = polyphase(volts, rim_part)
        coarse = jnp.einsum('qbn,sfn->qbsf', coarse_tab, framed, precision=lax.Precision.HIGHEST)
        shaped = coarse.reshape(2, BANDS, STN_DEV, SPECTRA, NFINE)
        return channelize_packed(shaped, band_ids, delay_part, phase_part, flag_part)
    chans = lax.map(channelize, (voltages.reshape(blocks, STN_DEV, SAMPLES), delays.reshape(blocks, STN_DEV), phases.reshape(blocks, STN_DEV), flags.reshape(blocks, STN_DEV)))
    chans = chans.transpose(1, 0, 2, 3).reshape(GROUPS, STREAMS, 2 * AVG * SPECTRA)
    factor = 1.0 / (SPECTRA * AVG)

    def correlate(block):
        return packed_gram(block, 1, factor)
    return lax.map(correlate, chans)
```

```python
import math

import jax
import jax.numpy as jnp
import numpy as np
from jax import lax
from jax.experimental import pallas as pl
from jax.experimental.pallas import tpu as pltpu
from jax.sharding import PartitionSpec as P

NFFT = 512
TAPS = 4
NFINE = 64
AVG = 4
BANDS = 32
STN = 32
SPEC = 4
FRAMES = SPEC * NFINE
RIM = (TAPS - 1) * NFFT
CHUNK = 16
TURN = NFFT * NFINE
F32 = jnp.float32
BF16 = jnp.bfloat16


def split_two(table):
    high = table.astype(jnp.bfloat16)
    low = (table - high.astype(np.float64)).astype(jnp.bfloat16)
    return high, low


def coarse_weights():
    length = TAPS * NFFT
    places = np.arange(length, dtype=np.float64)
    offsets = (places - length / 2 + 0.5) / NFFT
    taper = 0.54 - 0.46 * np.cos(2.0 * math.pi * places / (length - 1))
    window = (np.sinc(offsets) * taper).reshape(TAPS, NFFT)
    product = (np.arange(NFFT)[:, None] * (np.arange(BANDS) + 1)[None, :]) % NFFT
    angles = product * (2.0 * math.pi / NFFT)
    table = np.concatenate([np.cos(angles), -np.sin(angles)], 1) / math.sqrt(NFFT)
    taps = [np.concatenate(split_two(window[t][:, None] * table), 1) for t in range(TAPS)]
    return np.block([[taps[0], taps[1]], [taps[2], taps[3]]])


def fine_weights():
    product = (np.arange(NFINE)[:, None] * (np.arange(NFINE) - NFINE // 2)[None, :]) % NFINE
    angles = product * (2.0 * math.pi / NFINE)
    cosine = np.cos(angles) / math.sqrt(NFINE)
    sine = np.sin(angles) / math.sqrt(NFINE)
    full = np.zeros((2, 2, 2, NFINE, 4, 2, 4, 4, SPEC))
    pair = {(0, 0): cosine, (0, 1): -sine, (1, 0): sine, (1, 1): cosine}
    for (part_in, part_out), table in pair.items():
        for p in range(SPEC):
            full[p % 2, part_in, p // 2, :, :, part_out, :, :, p] = table.reshape(NFINE, 4, 4, 4)
    high, low = split_two(full.reshape(8 * NFINE, 512))
    return np.concatenate([high, low], 0)


def channel_kernel(
    volt_hbm, rim_hbm, w_ref, g_ref, ac_ref, as_ref, bc_ref, bs_ref, out_ref, xbuf, cbuf, dbuf, sems
):
    def copy(c):
        width = CHUNK * NFFT
        return pltpu.make_async_copy(
            volt_hbm.at[:, pl.ds(c * width, width)], xbuf.at[:, pl.ds(c * width, width)], sems.at[c]
        )

    rim_copy = pltpu.make_async_copy(
        rim_hbm, xbuf.at[:, pl.ds(FRAMES * NFFT, RIM)], sems.at[16]
    )
    for c in (0, 1, 4, 5, 2, 6, 3, 7, 8, 9, 12, 13, 10, 14, 11, 15):
        copy(c).start()
    rim_copy.start()
    lane = lax.broadcasted_iota(jnp.int32, (CHUNK * STN, 128), 1)
    first_half = lane < 64

    def spectrum(base):
        def frame(j):
            return xbuf[:, pl.ds(pl.multiple_of((base + j) * NFFT, NFFT), NFFT)]

        frames = [frame(j) for j in range(CHUNK + 3)]
        left = jnp.concatenate(frames[: CHUNK + 1], 0)
        right = jnp.concatenate(frames[2:], 0)
        both = jnp.concatenate([left, right], 1)
        z = jnp.dot(both, w_ref[...], preferred_element_type=F32)
        y = z[: CHUNK * STN, :128] + z[STN:, 128:]
        return y + pltpu.roll(y, 64, 1)

    @pl.loop(0, 8)
    def _(i):
        half = i // 4
        part = i % 4
        a = half * 8 + part

        @pl.when(i == 0)
        def _():
            copy(0).wait()

        @pl.when(part == 0)
        def _():
            copy(a + 4).wait()

        @pl.when(part < 3)
        def _():
            copy(a + 1).wait()

        @pl.when(i < 7)
        def _():
            copy(a + 5).wait()

        @pl.when(i == 7)
        def _():
            rim_copy.wait()

        s0 = spectrum(a * CHUNK)
        s1 = spectrum((a + 4) * CHUNK)
        value = jnp.where(first_half, s0, s1)
        other = jnp.where(first_half, pltpu.roll(s0, 32, 1), pltpu.roll(s1, 32, 1))
        cosine = jnp.concatenate([ac_ref[...]] * CHUNK, 0)
        sine = jnp.concatenate([as_ref[...]] * CHUNK, 0)
        row = pl.multiple_of(i * CHUNK * STN, CHUNK * STN)
        cbuf[pl.ds(row, CHUNK * STN), :] = value * cosine + other * sine

    for s in range(STN):
        turned = cbuf[pl.ds(s, 2 * NFINE, stride=STN), :].T
        dbuf[pl.ds(s, 128, stride=STN), :] = turned

    weights = jnp.concatenate([g_ref[:512, :], g_ref[:512, :], g_ref[512:, :]], 0)
    rows = 512

    for h in range(1024 // rows):
        data = jnp.concatenate([dbuf[x * 1024 + h * rows : x * 1024 + (h + 1) * rows, :] for x in range(4)], 1)
        high = data.astype(BF16)
        low = (data - high.astype(F32)).astype(BF16)
        z = jnp.dot(jnp.concatenate([high, low, high], 1), weights, preferred_element_type=F32)
        per = rows // STN
        for kh in range(4):
            piece = z[:, kh * 128 : (kh + 1) * 128]
            cosine = jnp.concatenate([bc_ref[:, kh * 128 : (kh + 1) * 128]] * per, 0)
            sine = jnp.concatenate([bs_ref[:, kh * 128 : (kh + 1) * 128]] * per, 0)
            result = (piece * cosine + pltpu.roll(piece, 64, 1) * sine).astype(BF16)
            for j in range(per):
                out_ref[(h * per + j) * 4 + kh] = result[j * STN : (j + 1) * STN]


def channelize(voltages, rim, ac, asn, bc, bs):
    vm = pl.BlockSpec(memory_space=pltpu.VMEM)
    hbm = pl.BlockSpec(memory_space=pl.ANY)
    return pl.pallas_call(
        channel_kernel,
        out_shape=jax.ShapeDtypeStruct((128, STN, 128), BF16),
        in_specs=[hbm, hbm, vm, vm, vm, vm, vm, vm],
        out_specs=vm,
        scratch_shapes=[
            pltpu.VMEM((STN, FRAMES * NFFT + RIM), BF16),
            pltpu.VMEM((2 * NFINE * STN, 128), F32),
            pltpu.VMEM((128 * STN, 128), F32),
            pltpu.SemaphoreType.DMA((17,)),
        ],
        name="channelize",
    )(voltages, rim, jnp.asarray(coarse_weights()), jnp.asarray(fine_weights()), ac, asn, bc, bs)


def correlate_kernel(r_ref, out_ref, x_buf, s_buf):
    group = pl.program_id(0)
    block = pl.program_id(1)

    for g in range(4):

        @pl.when((block == 0) & (group == g))
        def _():
            rows = 256
            lane = lax.broadcasted_iota(jnp.int32, (rows, 128), 1)
            place = (lane // 16) % 4
            sign = jnp.where(lane < 64, -1.0, 1.0)
            for n in range(1024 // rows):
                value = None
                for t in range(4):
                    start = t * 32 + n * rows // STN
                    src = r_ref[start : start + rows // STN].reshape(rows, 128).astype(F32)
                    shift = (16 * (t - g)) % 128
                    moved = pltpu.roll(src, shift, 1) if shift else src
                    value = moved if value is None else jnp.where(place == t, moved, value)
                x_buf[n * rows : (n + 1) * rows, :] = value.astype(BF16)
                s_buf[n * rows : (n + 1) * rows, :] = (pltpu.roll(value, 64, 1) * sign).astype(BF16)

    def product(left, right):
        return lax.dot_general(left, right, (((1,), (1,)), ((), ())), preferred_element_type=F32)

    for i in range(4):

        @pl.when(block == i)
        def _():
            mine = x_buf[i * 256 : (i + 1) * 256, :]
            if i > 0:
                out_ref[0, :, : i * 256] = product(mine, s_buf[: i * 256, :])
            if i < 3:
                out_ref[0, :, (i + 1) * 256 :] = product(mine, x_buf[(i + 1) * 256 :, :])
            real = product(mine, mine)
            imag = product(mine, s_buf[i * 256 : (i + 1) * 256, :])
            row = lax.broadcasted_iota(jnp.int32, (256, 256), 0)
            col = lax.broadcasted_iota(jnp.int32, (256, 256), 1)
            out_ref[0, :, i * 256 : (i + 1) * 256] = jnp.where(col >= row, real, imag)


def correlate(received):
    return pl.pallas_call(
        correlate_kernel,
        out_shape=jax.ShapeDtypeStruct((4, 1024, 1024), F32),
        grid=(4, 4),
        in_specs=[pl.BlockSpec(memory_space=pltpu.VMEM)],
        out_specs=pl.BlockSpec((1, 256, 1024), lambda g, i: (g, i, 0)),
        scratch_shapes=[pltpu.VMEM((1024, 128), BF16), pltpu.VMEM((1024, 128), BF16)],
        name="correlate",
    )(received)


def rotations(delays, phases, flags):
    def turn(index):
        angles = jnp.mod(index, TURN).astype(F32) * (-2.0 * math.pi / TURN)
        return jnp.cos(angles), jnp.sin(angles)

    lane = jnp.arange(128, dtype=jnp.int32)[None, :]
    band = lane % 32
    sign = jnp.where((lane // 32) % 2 == 0, -1.0, 1.0)
    cosine, sine = turn(delays[:, None] * ((band + 1) * NFINE) + phases[:, None])
    keep = flags.astype(F32)[:, None] * 0.125
    ac = cosine * keep
    asn = sine * keep * sign
    lane = jnp.arange(512, dtype=jnp.int32)[None, :]
    fine_id = (lane // 128) * 16 + (lane % 64) // 4
    sign = jnp.where((lane // 64) % 2 == 0, -1.0, 1.0)
    bc, sine = turn(delays[:, None] * (fine_id - NFINE // 2))
    return ac, asn, bc, sine * sign


def local(voltages, delays, phases, flags):
    rim = lax.ppermute(voltages[:, :RIM], "tm", [(1, 0), (2, 1), (3, 2)])
    sent = channelize(voltages, rim, *rotations(delays, phases, flags))
    received = lax.all_to_all(sent, ("tm", "stn"), 0, 0, tiled=True)
    return correlate(received)


def solution(mesh):
    in_specs = (P("stn", "tm"), P("stn"), P("stn"), P("stn"))
    out_specs = P(("tm", "stn"), None, None)
    return jax.shard_map(local, mesh=mesh, in_specs=in_specs, out_specs=out_specs, check_vma=False)
```

```python
import math

import jax
import jax.numpy as jnp
import numpy as np
from jax import lax
from jax.experimental import pallas as pl
from jax.experimental.pallas import tpu as pltpu
from jax.sharding import PartitionSpec as P

NFFT = 512
TAPS = 4
NFINE = 64
AVG = 4
BANDS = 32
STN = 32
SPEC = 4
FRAMES = SPEC * NFINE
RIM = (TAPS - 1) * NFFT
CHUNK = 16
TURN = NFFT * NFINE
F32 = jnp.float32
BF16 = jnp.bfloat16


def split_two(table):
    high = table.astype(jnp.bfloat16)
    low = (table - high.astype(np.float64)).astype(jnp.bfloat16)
    return high, low


def coarse_weights():
    length = TAPS * NFFT
    places = np.arange(length, dtype=np.float64)
    offsets = (places - length / 2 + 0.5) / NFFT
    taper = 0.54 - 0.46 * np.cos(2.0 * math.pi * places / (length - 1))
    window = (np.sinc(offsets) * taper).reshape(TAPS, NFFT)
    product = (np.arange(NFFT)[:, None] * (np.arange(BANDS) + 1)[None, :]) % NFFT
    angles = product * (2.0 * math.pi / NFFT)
    table = np.concatenate([np.cos(angles), -np.sin(angles)], 1) / math.sqrt(NFFT)
    taps = [np.concatenate(split_two(window[t][:, None] * table), 1) for t in range(TAPS)]
    return np.block([[taps[0], taps[1]], [taps[2], taps[3]]])


def fine_weights():
    product = (np.arange(NFINE)[:, None] * (np.arange(NFINE) - NFINE // 2)[None, :]) % NFINE
    angles = product * (2.0 * math.pi / NFINE)
    cosine = np.cos(angles) / math.sqrt(NFINE)
    sine = np.sin(angles) / math.sqrt(NFINE)
    full = np.zeros((2, 2, 2, NFINE, 4, 2, 4, 4, SPEC))
    pair = {(0, 0): cosine, (0, 1): -sine, (1, 0): sine, (1, 1): cosine}
    for (part_in, part_out), table in pair.items():
        for p in range(SPEC):
            full[p % 2, part_in, p // 2, :, :, part_out, :, :, p] = table.reshape(NFINE, 4, 4, 4)
    high, low = split_two(full.reshape(8 * NFINE, 512))
    return np.concatenate([high, low], 0)


def channel_kernel(
    volt_hbm, rim_hbm, w_ref, g_ref, ac_ref, as_ref, bc_ref, bs_ref, out_ref, xbuf, cbuf, dbuf, sems
):
    def copy(c):
        width = CHUNK * NFFT
        return pltpu.make_async_copy(
            volt_hbm.at[:, pl.ds(c * width, width)], xbuf.at[:, pl.ds(c * width, width)], sems.at[c]
        )

    rim_copy = pltpu.make_async_copy(
        rim_hbm, xbuf.at[:, pl.ds(FRAMES * NFFT, RIM)], sems.at[16]
    )
    for c in (0, 1, 4, 5, 2, 6, 3, 7, 8, 9, 12, 13, 10, 14, 11, 15):
        copy(c).start()
    rim_copy.start()
    lane = lax.broadcasted_iota(jnp.int32, (CHUNK * STN, 128), 1)
    first_half = lane < 64

    def spectrum(base):
        def frame(j):
            return xbuf[:, pl.ds(pl.multiple_of((base + j) * NFFT, NFFT), NFFT)]

        frames = [frame(j) for j in range(CHUNK + 3)]
        left = jnp.concatenate(frames[: CHUNK + 1], 0)
        right = jnp.concatenate(frames[2:], 0)
        both = jnp.concatenate([left, right], 1)
        z = jnp.dot(both, w_ref[...], preferred_element_type=F32)
        y = z[: CHUNK * STN, :128] + z[STN:, 128:]
        return y + pltpu.roll(y, 64, 1)

    @pl.loop(0, 8)
    def _(i):
        half = i // 4
        part = i % 4
        a = half * 8 + part

        @pl.when(i == 0)
        def _():
            copy(0).wait()

        @pl.when(part == 0)
        def _():
            copy(a + 4).wait()

        @pl.when(part < 3)
        def _():
            copy(a + 1).wait()

        @pl.when(i < 7)
        def _():
            copy(a + 5).wait()

        @pl.when(i == 7)
        def _():
            rim_copy.wait()

        s0 = spectrum(a * CHUNK)
        s1 = spectrum((a + 4) * CHUNK)
        value = jnp.where(first_half, s0, s1)
        other = jnp.where(first_half, pltpu.roll(s0, 32, 1), pltpu.roll(s1, 32, 1))
        cosine = jnp.concatenate([ac_ref[...]] * CHUNK, 0)
        sine = jnp.concatenate([as_ref[...]] * CHUNK, 0)
        row = pl.multiple_of(i * CHUNK * STN, CHUNK * STN)
        cbuf[pl.ds(row, CHUNK * STN), :] = value * cosine + other * sine

    for s in range(STN):
        turned = cbuf[pl.ds(s, 2 * NFINE, stride=STN), :].T
        dbuf[pl.ds(s, 128, stride=STN), :] = turned

    weights = jnp.concatenate([g_ref[:512, :], g_ref[:512, :], g_ref[512:, :]], 0)
    rows = 512

    for h in range(1024 // rows):
        data = jnp.concatenate([dbuf[x * 1024 + h * rows : x * 1024 + (h + 1) * rows, :] for x in range(4)], 1)
        high = data.astype(BF16)
        low = (data - high.astype(F32)).astype(BF16)
        z = jnp.dot(jnp.concatenate([high, low, high], 1), weights, preferred_element_type=F32)
        per = rows // STN
        for kh in range(4):
            piece = z[:, kh * 128 : (kh + 1) * 128]
            cosine = jnp.concatenate([bc_ref[:, kh * 128 : (kh + 1) * 128]] * per, 0)
            sine = jnp.concatenate([bs_ref[:, kh * 128 : (kh + 1) * 128]] * per, 0)
            result = (piece * cosine + pltpu.roll(piece, 64, 1) * sine).astype(BF16)
            for j in range(per):
                out_ref[(h * per + j) * 4 + kh] = result[j * STN : (j + 1) * STN]


def channelize(voltages, rim, ac, asn, bc, bs):
    vm = pl.BlockSpec(memory_space=pltpu.VMEM)
    hbm = pl.BlockSpec(memory_space=pl.ANY)
    return pl.pallas_call(
        channel_kernel,
        out_shape=jax.ShapeDtypeStruct((128, STN, 128), BF16),
        in_specs=[hbm, hbm, vm, vm, vm, vm, vm, vm],
        out_specs=vm,
        scratch_shapes=[
            pltpu.VMEM((STN, FRAMES * NFFT + RIM), BF16),
            pltpu.VMEM((2 * NFINE * STN, 128), F32),
            pltpu.VMEM((128 * STN, 128), F32),
            pltpu.SemaphoreType.DMA((17,)),
        ],
        name="channelize",
    )(voltages, rim, jnp.asarray(coarse_weights()), jnp.asarray(fine_weights()), ac, asn, bc, bs)


def correlate_kernel(r_ref, out_hbm, x_buf, s_buf, o_buf, sems):
    rows = 128
    lane = lax.broadcasted_iota(jnp.int32, (rows, 128), 1)
    place = (lane // 16) % 4
    sign = jnp.where(lane < 64, -1.0, 1.0)

    def prepare(g, n):
        slot = g % 2
        value = None
        for t in range(4):
            start = t * 32 + n * rows // STN
            src = r_ref[start : start + rows // STN].reshape(rows, 128).astype(F32)
            shift = (16 * (t - g)) % 128
            moved = pltpu.roll(src, shift, 1) if shift else src
            value = moved if value is None else jnp.where(place == t, moved, value)
        x_buf[slot, n * rows : (n + 1) * rows, :] = value.astype(BF16)
        s_buf[slot, n * rows : (n + 1) * rows, :] = (pltpu.roll(value, 64, 1) * sign).astype(BF16)

    def product(left, right):
        return lax.dot_general(left, right, (((1,), (1,)), ((), ())), preferred_element_type=F32)

    def send(g, j):
        cols = pl.ds(j * 256, 256)
        return pltpu.make_async_copy(
            o_buf.at[g % 2, :, cols], out_hbm.at[g, :, cols], sems.at[g % 2, j]
        )

    row = lax.broadcasted_iota(jnp.int32, (256, 256), 0)
    upper = lax.broadcasted_iota(jnp.int32, (256, 256), 1) >= row
    for n in range(8):
        prepare(0, n)
    for g in range(4):
        slot = g % 2
        for j in range(4):
            low, high = j * 256, (j + 1) * 256
            if g >= 2:
                send(g - 2, j).wait()
            if g < 3:
                prepare(g + 1, 2 * j)
                prepare(g + 1, 2 * j + 1)
            real = product(x_buf[slot, :high, :], x_buf[slot, low:high, :])
            imag = product(x_buf[slot, low:, :], s_buf[slot, low:high, :])
            if j > 0:
                o_buf[slot, :low, low:high] = real[:low]
            if j < 3:
                o_buf[slot, high:, low:high] = imag[256:]
            o_buf[slot, low:high, low:high] = jnp.where(upper, real[low:], imag[:256])
            send(g, j).start()
    for g in (2, 3):
        for j in range(4):
            send(g, j).wait()


def correlate(received):
    return pl.pallas_call(
        correlate_kernel,
        out_shape=jax.ShapeDtypeStruct((4, 1024, 1024), F32),
        in_specs=[pl.BlockSpec(memory_space=pltpu.VMEM)],
        out_specs=pl.BlockSpec(memory_space=pl.ANY),
        scratch_shapes=[
            pltpu.VMEM((2, 1024, 128), BF16),
            pltpu.VMEM((2, 1024, 128), BF16),
            pltpu.VMEM((2, 1024, 1024), F32),
            pltpu.SemaphoreType.DMA((2, 4)),
        ],
        name="correlate",
    )(received)


def rotations(delays, phases, flags):
    def turn(index):
        angles = jnp.mod(index, TURN).astype(F32) * (-2.0 * math.pi / TURN)
        return jnp.cos(angles), jnp.sin(angles)

    lane = jnp.arange(128, dtype=jnp.int32)[None, :]
    band = lane % 32
    sign = jnp.where((lane // 32) % 2 == 0, -1.0, 1.0)
    cosine, sine = turn(delays[:, None] * ((band + 1) * NFINE) + phases[:, None])
    keep = flags.astype(F32)[:, None] * 0.125
    ac = cosine * keep
    asn = sine * keep * sign
    lane = jnp.arange(512, dtype=jnp.int32)[None, :]
    fine_id = (lane // 128) * 16 + (lane % 64) // 4
    sign = jnp.where((lane // 64) % 2 == 0, -1.0, 1.0)
    bc, sine = turn(delays[:, None] * (fine_id - NFINE // 2))
    return ac, asn, bc, sine * sign


def local(voltages, delays, phases, flags):
    rim = lax.ppermute(voltages[:, :RIM], "tm", [(1, 0), (2, 1), (3, 2)])
    sent = channelize(voltages, rim, *rotations(delays, phases, flags))
    received = lax.all_to_all(sent, ("tm", "stn"), 0, 0, tiled=True)
    return correlate(received)


def solution(mesh):
    in_specs = (P("stn", "tm"), P("stn"), P("stn"), P("stn"))
    out_specs = P(("tm", "stn"), None, None)
    return jax.shard_map(local, mesh=mesh, in_specs=in_specs, out_specs=out_specs, check_vma=False)
```

```python
import math

import jax
import jax.numpy as jnp
import numpy as np
from jax import lax
from jax.experimental import pallas as pl
from jax.experimental.pallas import tpu as pltpu
from jax.sharding import PartitionSpec as P

NFFT = 512
TAPS = 4
NFINE = 64
AVG = 4
BANDS = 32
STN = 32
SPEC = 4
FRAMES = SPEC * NFINE
RIM = (TAPS - 1) * NFFT
CHUNK = 16
WIDE = 32
TURN = NFFT * NFINE
F32 = jnp.float32
BF16 = jnp.bfloat16


def split_two(table):
    high = table.astype(jnp.bfloat16)
    low = (table - high.astype(np.float64)).astype(jnp.bfloat16)
    return high, low


def coarse_weights():
    length = TAPS * NFFT
    places = np.arange(length, dtype=np.float64)
    offsets = (places - length / 2 + 0.5) / NFFT
    taper = 0.54 - 0.46 * np.cos(2.0 * math.pi * places / (length - 1))
    window = (np.sinc(offsets) * taper).reshape(TAPS, NFFT)
    product = (np.arange(NFFT)[:, None] * (np.arange(BANDS) + 1)[None, :]) % NFFT
    angles = product * (2.0 * math.pi / NFFT)
    table = np.concatenate([np.cos(angles), -np.sin(angles)], 1) / math.sqrt(NFFT)
    taps = [np.concatenate(split_two(window[t][:, None] * table), 1) for t in range(TAPS)]
    return np.block([[taps[0], taps[1]], [taps[2], taps[3]]])


def fine_weights():
    product = (np.arange(NFINE)[:, None] * (np.arange(NFINE) - NFINE // 2)[None, :]) % NFINE
    angles = product * (2.0 * math.pi / NFINE)
    cosine = np.cos(angles) / math.sqrt(NFINE)
    sine = np.sin(angles) / math.sqrt(NFINE)
    full = np.zeros((2, 2, NFINE, 2, NFINE, 2))
    pair = {(0, 0): cosine, (0, 1): -sine, (1, 0): sine, (1, 1): cosine}
    for (part_in, part_out), table in pair.items():
        for p in range(2):
            full[part_in, p, :, part_out, :, p] = table
    high, low = split_two(full.reshape(4 * NFINE, 4 * NFINE))
    return np.concatenate([high, high, low], 0)


def send_moves():
    source = np.arange(512).reshape(4, 4, 32).transpose(1, 0, 2).reshape(-1)
    return np.eye(512)[:, source].astype(jnp.bfloat16)


def group_moves():
    source = np.arange(512).reshape(4, 2, 2, 4, 8).transpose(3, 1, 2, 0, 4).reshape(-1)
    return np.eye(512)[:, source].astype(jnp.bfloat16)


def channel_kernel(
    volt_hbm, rim_ref, w_ref, g_ref, m_ref, d_ref, p_ref, f_ref, out_ref, xbuf, cbuf, dbuf, tcos, tsin, sems
):
    def copy(c):
        width = CHUNK * NFFT
        return pltpu.make_async_copy(
            volt_hbm.at[:, pl.ds(c * width, width)], xbuf.at[:, pl.ds(c * width, width)], sems.at[c]
        )

    for c in (0, 1, 4, 5, 2, 6, 3, 7, 8, 9, 12, 13, 10, 14, 11, 15):
        copy(c).start()
    xbuf[:, FRAMES * NFFT :] = rim_ref[...]
    first_half = lax.broadcasted_iota(jnp.int32, (WIDE * STN, 128), 1) < 64
    diagonal = lax.broadcasted_iota(jnp.int32, (STN, STN), 0) == lax.broadcasted_iota(jnp.int32, (STN, STN), 1)

    def column(ref):
        spread = jnp.broadcast_to(ref[...].astype(F32), (STN, STN))
        picked = jnp.sum(jnp.where(diagonal, spread, 0.0), 1, keepdims=True)
        return jnp.broadcast_to(picked, (STN, 128))

    delay = column(d_ref).astype(jnp.int32)
    phase = column(p_ref).astype(jnp.int32)
    keep = column(f_ref) * 0.125
    fine_id = lax.broadcasted_iota(jnp.int32, (STN, 128), 1) // 2 - NFINE // 2

    def rotation(band):
        index = (delay * ((band + 1) * NFINE + fine_id) + phase) & (TURN - 1)
        quarter = (index + TURN // 8) >> 13
        angle = (index - (quarter << 13)).astype(F32) * (2.0 * math.pi / TURN)
        square = angle * angle
        sine = -1.9515295891e-4 * square + 8.3321608736e-3
        sine = (sine * square - 1.6666654611e-1) * square * angle + angle
        cosine = 2.443315711809948e-5 * square - 1.388731625493765e-3
        cosine = (cosine * square + 4.166664568298827e-2) * square * square - 0.5 * square + 1.0
        swap = (quarter & 1) == 1
        real = jnp.where(swap, sine, cosine) * keep
        imag = jnp.where(swap, cosine, sine) * keep
        real = jnp.where(((quarter + 1) & 2) == 2, -real, real)
        imag = jnp.where((quarter & 2) == 2, -imag, imag)
        row = pl.multiple_of(band * STN, STN)
        tcos[pl.ds(row, STN), :] = real
        tsin[pl.ds(row, STN), :] = imag

    def spectrum(base):
        def frame(j):
            return xbuf[:, pl.ds(pl.multiple_of((base + j) * NFFT, NFFT), NFFT)]

        frames = [frame(j) for j in range(WIDE + 3)]
        left = jnp.concatenate(frames[: WIDE + 1], 0)
        right = jnp.concatenate(frames[2:], 0)
        both = jnp.concatenate([left, right], 1)
        z = jnp.dot(both, w_ref[...], preferred_element_type=F32)
        return z[: WIDE * STN, :128] + z[STN:, 128:]

    @pl.loop(0, 4)
    def _(i):
        part = i % 2
        a = (i // 2) * 8 + part * 2

        @pl.when(i == 0)
        def _():
            copy(0).wait()

        @pl.when(part == 0)
        def _():
            for c in (1, 2, 4, 5, 6):
                copy(a + c).wait()

        @pl.when(part == 1)
        def _():
            for c in (1, 5):
                copy(a + c).wait()

        @pl.when(i == 1)
        def _():
            copy(8).wait()

        y0 = spectrum(a * CHUNK)
        y1 = spectrum((a + 4) * CHUNK)
        value = jnp.where(first_half, y0, y1) + pltpu.roll(jnp.where(first_half, y1, y0), 64, 1)
        cbuf[pl.ds(pl.multiple_of(i * WIDE, WIDE), WIDE)] = value.reshape(WIDE, STN, 128)
        for j in range(8):
            rotation(i * 8 + j)

    for sb in range(4):
        streams = jnp.swapaxes(cbuf[:, sb * 8 : (sb + 1) * 8, :], 0, 1)
        turned = jnp.stack([streams[s].T for s in range(8)], 0)
        dbuf[:, sb * 8 : (sb + 1) * 8, :] = jnp.swapaxes(turned, 0, 1)

    per = 16
    rows = per * STN
    for h in range(BANDS // per):
        reals, imags = [], []
        cosine = tcos[h * rows : (h + 1) * rows, :]
        sine = tsin[h * rows : (h + 1) * rows, :]
        for p in range(2):
            starts = [(p * 2 + q) * BANDS + h * per for q in range(2)]
            data = jnp.concatenate([dbuf[x : x + per].reshape(rows, 128) for x in starts], 1)
            high = data.astype(BF16)
            low = (data - high.astype(F32)).astype(BF16)
            z = jnp.dot(jnp.concatenate([high, low, high], 1), g_ref[...], preferred_element_type=F32)
            reals.append((z[:, :128] * cosine + z[:, 128:] * sine).astype(BF16))
            imags.append((z[:, 128:] * cosine - z[:, :128] * sine).astype(BF16))
        moved = jnp.dot(jnp.concatenate(reals + imags, 1), m_ref[...], preferred_element_type=F32).astype(BF16)
        for j in range(per):
            for kh in range(4):
                out_ref[(h * per + j) * 4 + kh] = moved[j * STN : (j + 1) * STN, kh * 128 : (kh + 1) * 128]


def channelize(voltages, rim, delays, phases, flags):
    vm = pl.BlockSpec(memory_space=pltpu.VMEM)
    hbm = pl.BlockSpec(memory_space=pl.ANY)
    return pl.pallas_call(
        channel_kernel,
        out_shape=jax.ShapeDtypeStruct((128, STN, 128), BF16),
        in_specs=[hbm] + [vm] * 7,
        out_specs=vm,
        scratch_shapes=[
            pltpu.VMEM((STN, FRAMES * NFFT + RIM), BF16),
            pltpu.VMEM((2 * NFINE, STN, 128), F32),
            pltpu.VMEM((128, STN, 128), F32),
            pltpu.VMEM((BANDS * STN, 128), F32),
            pltpu.VMEM((BANDS * STN, 128), F32),
            pltpu.SemaphoreType.DMA((16,)),
        ],
        name="channelize",
    )(
        voltages,
        rim,
        jnp.asarray(coarse_weights()),
        jnp.asarray(fine_weights()),
        jnp.asarray(send_moves()),
        delays.reshape(1, STN),
        phases.reshape(1, STN),
        flags.reshape(1, STN),
    )


def correlate_kernel(r_ref, m_ref, out_hbm, x_buf, s_buf, o_buf, sems):
    sign = jnp.where(lax.broadcasted_iota(jnp.int32, (1024, 128), 1) < 64, 1.0, -1.0)

    def prepare(pair):
        parts = [r_ref[t * STN : (t + 1) * STN].reshape(1024, 128) for t in range(4)]
        both = jnp.dot(
            jnp.concatenate(parts, 1), m_ref[:, pair * 256 : (pair + 1) * 256], preferred_element_type=F32
        )
        for k in range(2):
            value = both[:, k * 128 : (k + 1) * 128]
            x_buf[pair * 2 + k] = value.astype(BF16)
            s_buf[pair * 2 + k] = (pltpu.roll(value, 64, 1) * sign).astype(BF16)

    def product(left, right):
        return lax.dot_general(left, right, (((1,), (1,)), ((), ())), preferred_element_type=F32)

    def send(g, j):
        cols = pl.ds(j * 256, 256)
        return pltpu.make_async_copy(o_buf.at[g, :, cols], out_hbm.at[g, :, cols], sems.at[g, j])

    row = lax.broadcasted_iota(jnp.int32, (256, 256), 0)
    upper = lax.broadcasted_iota(jnp.int32, (256, 256), 1) >= row
    prepare(0)
    for g in range(4):
        for j in range(4):
            low, high = j * 256, (j + 1) * 256
            column = x_buf[g, low:high, :]
            real = product(x_buf[g, :high, :], column)
            imag = product(s_buf[g, low:, :], column)
            if j > 0:
                o_buf[g, :low, low:high] = real[:low]
            if j < 3:
                o_buf[g, high:, low:high] = imag[256:]
            o_buf[g, low:high, low:high] = jnp.where(upper, real[low:], imag[:256])
            send(g, j).start()
        if g == 0:
            prepare(1)
    for g in range(4):
        for j in range(4):
            send(g, j).wait()


def correlate(received):
    return pl.pallas_call(
        correlate_kernel,
        out_shape=jax.ShapeDtypeStruct((4, 1024, 1024), F32),
        in_specs=[pl.BlockSpec(memory_space=pltpu.VMEM)] * 2,
        out_specs=pl.BlockSpec(memory_space=pl.ANY),
        scratch_shapes=[
            pltpu.VMEM((4, 1024, 128), BF16),
            pltpu.VMEM((4, 1024, 128), BF16),
            pltpu.VMEM((4, 1024, 1024), F32),
            pltpu.SemaphoreType.DMA((4, 4)),
        ],
        name="correlate",
    )(received, jnp.asarray(group_moves()))


def local(voltages, delays, phases, flags):
    rim = lax.ppermute(voltages[:, :RIM], "tm", [(1, 0), (2, 1), (3, 2)])
    sent = channelize(voltages, rim, delays, phases, flags)
    received = lax.all_to_all(sent, ("tm", "stn"), 0, 0, tiled=True)
    return correlate(received)


def solution(mesh):
    in_specs = (P("stn", "tm"), P("stn"), P("stn"), P("stn"))
    out_specs = P(("tm", "stn"), None, None)
    return jax.shard_map(local, mesh=mesh, in_specs=in_specs, out_specs=out_specs, check_vma=False)
```

```python
import math

import jax
import jax.numpy as jnp
import numpy as np
from jax import lax
from jax.experimental import pallas as pl
from jax.experimental.pallas import tpu as pltpu
from jax.sharding import PartitionSpec as P

NFFT = 512
TAPS = 4
NFINE = 64
AVG = 4
BANDS = 32
STN = 32
SPEC = 4
FRAMES = SPEC * NFINE
RIM = (TAPS - 1) * NFFT
CHUNK = 16
WIDE = 32
LIMIT = 40 * 2**20
TURN = NFFT * NFINE
F32 = jnp.float32
BF16 = jnp.bfloat16


def split_two(table):
    high = table.astype(jnp.bfloat16)
    low = (table - high.astype(np.float64)).astype(jnp.bfloat16)
    return high, low


def coarse_weights():
    length = TAPS * NFFT
    places = np.arange(length, dtype=np.float64)
    offsets = (places - length / 2 + 0.5) / NFFT
    taper = 0.54 - 0.46 * np.cos(2.0 * math.pi * places / (length - 1))
    window = (np.sinc(offsets) * taper).reshape(TAPS, NFFT)
    product = (np.arange(NFFT)[:, None] * (np.arange(BANDS) + 1)[None, :]) % NFFT
    angles = product * (2.0 * math.pi / NFFT)
    table = np.concatenate([np.cos(angles), -np.sin(angles)], 1) / math.sqrt(NFFT)
    taps = [np.concatenate(split_two(window[t][:, None] * table), 1) for t in range(TAPS)]
    return np.block([[taps[0], taps[1]], [taps[2], taps[3]]])


def fine_weights():
    product = (np.arange(NFINE)[:, None] * (np.arange(NFINE) - NFINE // 2)[None, :]) % NFINE
    angles = product * (2.0 * math.pi / NFINE)
    cosine = np.cos(angles) / math.sqrt(NFINE)
    sine = np.sin(angles) / math.sqrt(NFINE)
    full = np.zeros((2, 2, NFINE, 2, NFINE, 2))
    pair = {(0, 0): cosine, (0, 1): -sine, (1, 0): sine, (1, 1): cosine}
    for (part_in, part_out), table in pair.items():
        for p in range(2):
            full[part_in, p, :, part_out, :, p] = table
    high, low = split_two(full.reshape(4 * NFINE, 4 * NFINE))
    return np.concatenate([high, high, low], 0)


def send_moves():
    source = np.arange(512).reshape(4, 4, 32).transpose(1, 0, 2).reshape(-1)
    return np.eye(512)[:, source].astype(jnp.bfloat16)


def group_moves():
    source = np.arange(512).reshape(4, 2, 2, 4, 8).transpose(3, 1, 2, 0, 4).reshape(-1)
    return np.eye(512)[:, source].astype(jnp.bfloat16)


def coarse_kernel(
    volt_hbm, w_hbm, d_hbm, p_hbm, f_hbm, cbuf, tcos, tsin, w_ref, xbuf, small, sems, tsems
):
    def copy(c):
        width = CHUNK * NFFT
        return pltpu.make_async_copy(
            volt_hbm.at[:, pl.ds(c * width, width)], xbuf.at[:, pl.ds(c * width, width)], sems.at[c]
        )

    early = (0, 1, 2, 4, 5, 6)
    late = (3, 7, 8, 9, 10, 12, 13, 14, 11, 15)
    streams = [
        pltpu.make_async_copy(source, small.at[k], tsems.at[k]) for k, source in enumerate((d_hbm, p_hbm, f_hbm))
    ]
    for each in streams:
        each.start()
    weights = pltpu.make_async_copy(w_hbm, w_ref, tsems.at[3])
    weights.start()
    for c in early:
        copy(c).start()
    xbuf[:, FRAMES * NFFT :] = jnp.zeros((STN, RIM), BF16)
    first_half = lax.broadcasted_iota(jnp.int32, (WIDE * STN, 128), 1) < 64
    diagonal = lax.broadcasted_iota(jnp.int32, (STN, STN), 0) == lax.broadcasted_iota(jnp.int32, (STN, STN), 1)

    def column(ref):
        spread = jnp.broadcast_to(ref[...].astype(F32), (STN, STN))
        picked = jnp.sum(jnp.where(diagonal, spread, 0.0), 1, keepdims=True)
        return jnp.broadcast_to(picked, (STN, 128))

    for each in streams:
        each.wait()
    delay = column(small.at[0]).astype(jnp.int32)
    phase = column(small.at[1]).astype(jnp.int32)
    keep = column(small.at[2]) * 0.125
    fine_id = lax.broadcasted_iota(jnp.int32, (STN, 128), 1) // 2 - NFINE // 2

    def rotation(band):
        index = (delay * ((band + 1) * NFINE + fine_id) + phase) & (TURN - 1)
        quarter = (index + TURN // 8) >> 13
        angle = (index - (quarter << 13)).astype(F32) * (2.0 * math.pi / TURN)
        square = angle * angle
        sine = -1.9515295891e-4 * square + 8.3321608736e-3
        sine = (sine * square - 1.6666654611e-1) * square * angle + angle
        cosine = 2.443315711809948e-5 * square - 1.388731625493765e-3
        cosine = (cosine * square + 4.166664568298827e-2) * square * square - 0.5 * square + 1.0
        swap = (quarter & 1) == 1
        real = jnp.where(swap, sine, cosine) * keep
        imag = jnp.where(swap, cosine, sine) * keep
        real = jnp.where(((quarter + 1) & 2) == 2, -real, real)
        imag = jnp.where((quarter & 2) == 2, -imag, imag)
        tcos[band] = real
        tsin[band] = imag

    def spectrum(base):
        def frame(j):
            return xbuf[:, pl.ds(pl.multiple_of((base + j) * NFFT, NFFT), NFFT)]

        frames = [frame(j) for j in range(WIDE + 3)]
        left = jnp.concatenate(frames[: WIDE + 1], 0)
        right = jnp.concatenate(frames[2:], 0)
        both = jnp.concatenate([left, right], 1)
        z = jnp.dot(both, w_ref[...], preferred_element_type=F32)
        return z[: WIDE * STN, :128] + z[STN:, 128:]

    @pl.loop(0, 4)
    def _(i):
        part = i % 2
        a = (i // 2) * 8 + part * 2

        @pl.when(i == 0)
        def _():
            weights.wait()
            for c in early:
                copy(c).wait()
            for c in late:
                copy(c).start()

        @pl.when(i == 2)
        def _():
            for c in (9, 10, 12, 13, 14):
                copy(c).wait()

        @pl.when(part == 1)
        def _():
            for c in (1, 5):
                copy(a + c).wait()

        @pl.when(i == 1)
        def _():
            copy(8).wait()

        y0 = spectrum(a * CHUNK)
        y1 = spectrum((a + 4) * CHUNK)
        value = jnp.where(first_half, y0, y1) + pltpu.roll(jnp.where(first_half, y1, y0), 64, 1)
        cbuf[pl.ds(pl.multiple_of(i * WIDE, WIDE), WIDE)] = value.reshape(WIDE, STN, 128)
        for j in range(8):
            rotation(i * 8 + j)


def fine_kernel(
    c_ref, rim_ref, w_ref, tcos, tsin, g_hbm, m_hbm, out_hbm, g_ref, m_ref, dbuf0, dbuf1, obuf0, obuf1, tsems
):
    tables = [
        pltpu.make_async_copy(source, target, tsems.at[k])
        for k, (source, target) in enumerate(((g_hbm, g_ref), (m_hbm, m_ref)))
    ]
    tables[0].start()
    tables[1].start()
    none = jnp.zeros((STN, NFFT), BF16)
    rim = [rim_ref[:, k * NFFT : (k + 1) * NFFT] for k in range(TAPS - 1)]
    left = jnp.concatenate([none, none, none, rim[0]], 0)
    right = jnp.concatenate([none] + rim, 0)
    z = jnp.dot(jnp.concatenate([left, right], 1), w_ref[...], preferred_element_type=F32)
    y = z[: 3 * STN, :128] + z[STN:, 128:]
    second_half = lax.broadcasted_iota(jnp.int32, (3 * STN, 128), 1) >= 64
    extra = jnp.where(second_half, y + pltpu.roll(y, 64, 1), 0.0).reshape(3, STN, 128)
    last = 2 * NFINE - 3
    part = STN // 2
    rows = BANDS * part

    def reorder(h, dbuf):
        for sb in range(2):
            start = h * part + sb * 8
            ending = c_ref[last:, start : start + 8, :] + extra[:, start : start + 8, :]
            block = jnp.concatenate([c_ref[:last, start : start + 8, :], ending], 0)
            streams = jnp.swapaxes(block, 0, 1)
            turned = jnp.stack([streams[s].T for s in range(8)], 0)
            dbuf[:, sb * 8 : (sb + 1) * 8, :] = jnp.swapaxes(turned, 0, 1)

    def finish(h, dbuf, obuf):
        reals, imags = [], []
        cosine = tcos[:, h * part : (h + 1) * part, :].reshape(rows, 128)
        sine = tsin[:, h * part : (h + 1) * part, :].reshape(rows, 128)
        for p in range(2):
            starts = [(p * 2 + q) * BANDS for q in range(2)]
            data = jnp.concatenate([dbuf[x : x + BANDS].reshape(rows, 128) for x in starts], 1)
            high = data.astype(BF16)
            low = (data - high.astype(F32)).astype(BF16)
            z = jnp.dot(jnp.concatenate([high, low, high], 1), g_ref[...], preferred_element_type=F32)
            reals.append((z[:, :128] * cosine + z[:, 128:] * sine).astype(BF16))
            imags.append((z[:, 128:] * cosine - z[:, :128] * sine).astype(BF16))
        moved = jnp.dot(jnp.concatenate(reals + imags, 1), m_ref[...], preferred_element_type=F32).astype(BF16)
        for j in range(BANDS):
            for kh in range(4):
                obuf[j * 4 + kh] = moved[j * part : (j + 1) * part, kh * 128 : (kh + 1) * 128]

    def send(h, obuf):
        return pltpu.make_async_copy(obuf, out_hbm.at[:, pl.ds(h * part, part), :], tsems.at[2 + h])

    reorder(0, dbuf0)
    reorder(1, dbuf1)
    tables[0].wait()
    tables[1].wait()
    finish(0, dbuf0, obuf0)
    send(0, obuf0).start()
    finish(1, dbuf1, obuf1)
    send(1, obuf1).start()
    send(0, obuf0).wait()
    send(1, obuf1).wait()


def channelize(voltages, rim, delays, phases, flags):
    vm = pl.BlockSpec(memory_space=pltpu.VMEM)
    hbm = pl.BlockSpec(memory_space=pl.ANY)
    limits = pltpu.CompilerParams(vmem_limit_bytes=LIMIT)

    def near(array):
        return pltpu.with_memory_space_constraint(array, pltpu.VMEM)

    def far(array):
        return pltpu.with_memory_space_constraint(array, pltpu.HBM)

    block = pltpu.VMEM((2 * NFINE, STN, 128), F32)
    table = pltpu.VMEM((BANDS, STN, 128), F32)
    coarse, tcos, tsin, weights = pl.pallas_call(
        coarse_kernel,
        out_shape=[block, table, table, pltpu.VMEM((1024, 256), BF16)],
        in_specs=[hbm] * 5,
        out_specs=[vm] * 4,
        scratch_shapes=[
            pltpu.VMEM((STN, FRAMES * NFFT + RIM), BF16),
            pltpu.VMEM((3, 1, STN), jnp.int32),
            pltpu.SemaphoreType.DMA((16,)),
            pltpu.SemaphoreType.DMA((4,)),
        ],
        compiler_params=limits,
        name="coarse",
    )(
        far(voltages),
        far(jnp.asarray(coarse_weights())),
        far(delays.reshape(1, STN)),
        far(phases.reshape(1, STN)),
        far(flags.reshape(1, STN)),
    )
    half = (128, STN // 2, 128)
    return pl.pallas_call(
        fine_kernel,
        out_shape=jax.ShapeDtypeStruct((128, STN, 128), BF16),
        in_specs=[vm] * 5 + [hbm, hbm],
        out_specs=hbm,
        scratch_shapes=[
            pltpu.VMEM((768, 256), BF16),
            pltpu.VMEM((512, 512), BF16),
            pltpu.VMEM(half, F32),
            pltpu.VMEM(half, F32),
            pltpu.VMEM(half, BF16),
            pltpu.VMEM(half, BF16),
            pltpu.SemaphoreType.DMA((4,)),
        ],
        compiler_params=limits,
        name="fine",
    )(near(coarse), near(rim), near(weights), near(tcos), near(tsin), far(jnp.asarray(fine_weights())), far(jnp.asarray(send_moves())))


def correlate_kernel(r_ref, m_ref, out_hbm, x_buf, s_buf, o_buf, sems):
    sign = jnp.where(lax.broadcasted_iota(jnp.int32, (1024, 128), 1) < 64, 1.0, -1.0)

    def prepare(pair):
        parts = [r_ref[t * STN : (t + 1) * STN].reshape(1024, 128) for t in range(4)]
        both = jnp.dot(
            jnp.concatenate(parts, 1), m_ref[:, pair * 256 : (pair + 1) * 256], preferred_element_type=F32
        )
        for k in range(2):
            value = both[:, k * 128 : (k + 1) * 128]
            x_buf[pair * 2 + k] = value.astype(BF16)
            s_buf[pair * 2 + k] = (pltpu.roll(value, 64, 1) * sign).astype(BF16)

    def product(left, right):
        return lax.dot_general(left, right, (((1,), (1,)), ((), ())), preferred_element_type=F32)

    def send(g, j):
        cols = pl.ds(j * 256, 256)
        return pltpu.make_async_copy(o_buf.at[g, :, cols], out_hbm.at[g, :, cols], sems.at[g, j])

    row = lax.broadcasted_iota(jnp.int32, (256, 256), 0)
    upper = lax.broadcasted_iota(jnp.int32, (256, 256), 1) >= row
    prepare(0)
    for g in range(4):
        for j in range(4):
            low, high = j * 256, (j + 1) * 256
            column = x_buf[g, low:high, :]
            real = product(x_buf[g, :high, :], column)
            imag = product(s_buf[g, low:, :], column)
            if j > 0:
                o_buf[g, :low, low:high] = real[:low]
            if j < 3:
                o_buf[g, high:, low:high] = imag[256:]
            o_buf[g, low:high, low:high] = jnp.where(upper, real[low:], imag[:256])
            send(g, j).start()
        if g == 0:
            prepare(1)
    for g in range(4):
        for j in range(4):
            send(g, j).wait()


def correlate(received):
    return pl.pallas_call(
        correlate_kernel,
        out_shape=jax.ShapeDtypeStruct((4, 1024, 1024), F32),
        in_specs=[pl.BlockSpec(memory_space=pltpu.VMEM)] * 2,
        out_specs=pl.BlockSpec(memory_space=pl.ANY),
        scratch_shapes=[
            pltpu.VMEM((4, 1024, 128), BF16),
            pltpu.VMEM((4, 1024, 128), BF16),
            pltpu.VMEM((4, 1024, 1024), F32),
            pltpu.SemaphoreType.DMA((4, 4)),
        ],
        name="correlate",
    )(received, jnp.asarray(group_moves()))


def local(voltages, delays, phases, flags):
    rim = lax.ppermute(voltages[:, :RIM], "tm", [(1, 0), (2, 1), (3, 2)])
    sent = channelize(voltages, rim, delays, phases, flags)
    received = lax.all_to_all(sent, ("tm", "stn"), 0, 0, tiled=True)
    return correlate(received)


def solution(mesh):
    in_specs = (P("stn", "tm"), P("stn"), P("stn"), P("stn"))
    out_specs = P(("tm", "stn"), None, None)
    return jax.shard_map(local, mesh=mesh, in_specs=in_specs, out_specs=out_specs, check_vma=False)
```

```python
import math

import jax
import jax.numpy as jnp
import numpy as np
from jax import lax
from jax.experimental import pallas as pl
from jax.experimental.pallas import tpu as pltpu
from jax.sharding import PartitionSpec as P

NFFT = 512
TAPS = 4
NFINE = 64
AVG = 4
BANDS = 32
STN = 32
SPEC = 4
FRAMES = SPEC * NFINE
RIM = (TAPS - 1) * NFFT
CHUNK = 16
WIDE = 32
LIMIT = 40 * 2**20
TURN = NFFT * NFINE
F32 = jnp.float32
BF16 = jnp.bfloat16


def near(array):
    return pltpu.with_memory_space_constraint(array, pltpu.VMEM)


def far(array):
    return pltpu.with_memory_space_constraint(array, pltpu.HBM)


def split_two(table):
    high = table.astype(jnp.bfloat16)
    low = (table - high.astype(np.float64)).astype(jnp.bfloat16)
    return high, low


def coarse_weights():
    length = TAPS * NFFT
    places = np.arange(length, dtype=np.float64)
    offsets = (places - length / 2 + 0.5) / NFFT
    taper = 0.54 - 0.46 * np.cos(2.0 * math.pi * places / (length - 1))
    window = (np.sinc(offsets) * taper).reshape(TAPS, NFFT)
    product = (np.arange(NFFT)[:, None] * (np.arange(BANDS) + 1)[None, :]) % NFFT
    angles = product * (2.0 * math.pi / NFFT)
    table = np.concatenate([np.cos(angles), -np.sin(angles)], 1) / math.sqrt(NFFT)
    taps = [np.concatenate(split_two(window[t][:, None] * table), 1) for t in range(TAPS)]
    return np.block([[taps[0], taps[1]], [taps[2], taps[3]]])


def fine_weights():
    product = (np.arange(NFINE)[:, None] * (np.arange(NFINE) - NFINE // 2)[None, :]) % NFINE
    angles = product * (2.0 * math.pi / NFINE)
    cosine = np.cos(angles) / math.sqrt(NFINE)
    sine = np.sin(angles) / math.sqrt(NFINE)
    full = np.zeros((2, 2, NFINE, 2, NFINE, 2))
    pair = {(0, 0): cosine, (0, 1): -sine, (1, 0): sine, (1, 1): cosine}
    for (part_in, part_out), table in pair.items():
        for p in range(2):
            full[part_in, p, :, part_out, :, p] = table
    high, low = split_two(full.reshape(4 * NFINE, 4 * NFINE))
    return np.concatenate([high, high, low], 0)


def send_moves():
    source = np.arange(512).reshape(4, 4, 32).transpose(1, 0, 2).reshape(-1)
    return np.eye(512)[:, source].astype(jnp.bfloat16)


def group_moves():
    source = np.arange(512).reshape(4, 2, 2, 4, 8).transpose(3, 1, 2, 0, 4).reshape(-1)
    return np.eye(512)[:, source].astype(jnp.bfloat16)


def frames_copy(volt_hbm, xbuf, sem, start, count):
    where = pl.ds(start * NFFT, count * NFFT)
    return pltpu.make_async_copy(volt_hbm.at[:, where], xbuf.at[:, where], sem)


def first_kernel(volt_hbm, w_hbm, d_hbm, p_hbm, f_hbm, rim_ref, xbuf, w_ref, small, sems):
    copies = [pltpu.make_async_copy(volt_hbm.at[:, pl.ds(0, RIM)], rim_ref, sems.at[0])]
    for k, source in enumerate((d_hbm, p_hbm, f_hbm)):
        copies.append(pltpu.make_async_copy(source, small.at[k], sems.at[1 + k]))
    for k, start in enumerate((0, NFINE)):
        copies.append(frames_copy(volt_hbm, xbuf, sems.at[4 + k], start, WIDE + 3))
    copies.append(pltpu.make_async_copy(w_hbm, w_ref, sems.at[6]))
    for each in copies:
        each.start()
    xbuf[:, FRAMES * NFFT :] = jnp.zeros((STN, RIM), BF16)
    for each in copies:
        each.wait()


def coarse_kernel(volt_hbm, x_in, w_ref, small, cbuf, tcos, tsin, xbuf, sems):
    segments = ((35, 29), (99, 32), (131, 32), (192, 35), (163, 29), (227, 29))
    copies = [frames_copy(volt_hbm, xbuf, sems.at[k], *segment) for k, segment in enumerate(segments)]
    for each in copies:
        each.start()
    first_half = lax.broadcasted_iota(jnp.int32, (WIDE * STN, 128), 1) < 64
    diagonal = lax.broadcasted_iota(jnp.int32, (STN, STN), 0) == lax.broadcasted_iota(jnp.int32, (STN, STN), 1)

    def column(ref):
        spread = jnp.broadcast_to(ref[...].astype(F32), (STN, STN))
        picked = jnp.sum(jnp.where(diagonal, spread, 0.0), 1, keepdims=True)
        return jnp.broadcast_to(picked, (STN, 128))

    delay = column(small.at[0]).astype(jnp.int32)
    phase = column(small.at[1]).astype(jnp.int32)
    keep = column(small.at[2]) * 0.125
    fine_id = lax.broadcasted_iota(jnp.int32, (STN, 128), 1) // 2 - NFINE // 2

    def rotation(band):
        index = (delay * ((band + 1) * NFINE + fine_id) + phase) & (TURN - 1)
        quarter = (index + TURN // 8) >> 13
        angle = (index - (quarter << 13)).astype(F32) * (2.0 * math.pi / TURN)
        square = angle * angle
        sine = -1.9515295891e-4 * square + 8.3321608736e-3
        sine = (sine * square - 1.6666654611e-1) * square * angle + angle
        cosine = 2.443315711809948e-5 * square - 1.388731625493765e-3
        cosine = (cosine * square + 4.166664568298827e-2) * square * square - 0.5 * square + 1.0
        swap = (quarter & 1) == 1
        real = jnp.where(swap, sine, cosine) * keep
        imag = jnp.where(swap, cosine, sine) * keep
        real = jnp.where(((quarter + 1) & 2) == 2, -real, real)
        imag = jnp.where((quarter & 2) == 2, -imag, imag)
        tcos[band] = real
        tsin[band] = imag

    def spectrum(base):
        def frame(j):
            return xbuf[:, pl.ds(pl.multiple_of((base + j) * NFFT, NFFT), NFFT)]

        frames = [frame(j) for j in range(WIDE + 3)]
        left = jnp.concatenate(frames[: WIDE + 1], 0)
        right = jnp.concatenate(frames[2:], 0)
        both = jnp.concatenate([left, right], 1)
        z = jnp.dot(both, w_ref[...], preferred_element_type=F32)
        return z[: WIDE * STN, :128] + z[STN:, 128:]

    @pl.loop(0, 4)
    def _(i):
        part = i % 2
        a = (i // 2) * 8 + part * 2

        for k in range(3):

            @pl.when(i == k + 1)
            def _():
                copies[2 * k].wait()
                copies[2 * k + 1].wait()

        y0 = spectrum(a * CHUNK)
        y1 = spectrum((a + 4) * CHUNK)
        value = jnp.where(first_half, y0, y1) + pltpu.roll(jnp.where(first_half, y1, y0), 64, 1)
        cbuf[pl.ds(pl.multiple_of(i * WIDE, WIDE), WIDE)] = value.reshape(WIDE, STN, 128)
        for j in range(8):
            rotation(i * 8 + j)


def fine_kernel(
    c_ref, rim_ref, w_ref, tcos, tsin, g_hbm, m_hbm, out_hbm, g_ref, m_ref, dbuf0, dbuf1, obuf0, obuf1, tsems
):
    tables = [
        pltpu.make_async_copy(source, target, tsems.at[k])
        for k, (source, target) in enumerate(((g_hbm, g_ref), (m_hbm, m_ref)))
    ]
    tables[0].start()
    tables[1].start()
    none = jnp.zeros((STN, NFFT), BF16)
    rim = [rim_ref[:, k * NFFT : (k + 1) * NFFT] for k in range(TAPS - 1)]
    left = jnp.concatenate([none, none, none, rim[0]], 0)
    right = jnp.concatenate([none] + rim, 0)
    z = jnp.dot(jnp.concatenate([left, right], 1), w_ref[...], preferred_element_type=F32)
    y = z[: 3 * STN, :128] + z[STN:, 128:]
    second_half = lax.broadcasted_iota(jnp.int32, (3 * STN, 128), 1) >= 64
    extra = jnp.where(second_half, y + pltpu.roll(y, 64, 1), 0.0).reshape(3, STN, 128)
    last = 2 * NFINE - 3
    part = STN // 2
    rows = BANDS * part

    def reorder(h, dbuf):
        for sb in range(2):
            start = h * part + sb * 8
            ending = c_ref[last:, start : start + 8, :] + extra[:, start : start + 8, :]
            block = jnp.concatenate([c_ref[:last, start : start + 8, :], ending], 0)
            streams = jnp.swapaxes(block, 0, 1)
            turned = jnp.stack([streams[s].T for s in range(8)], 0)
            dbuf[:, sb * 8 : (sb + 1) * 8, :] = jnp.swapaxes(turned, 0, 1)

    def finish(h, dbuf, obuf):
        reals, imags = [], []
        cosine = tcos[:, h * part : (h + 1) * part, :].reshape(rows, 128)
        sine = tsin[:, h * part : (h + 1) * part, :].reshape(rows, 128)
        for p in range(2):
            starts = [(p * 2 + q) * BANDS for q in range(2)]
            data = jnp.concatenate([dbuf[x : x + BANDS].reshape(rows, 128) for x in starts], 1)
            high = data.astype(BF16)
            low = (data - high.astype(F32)).astype(BF16)
            z = jnp.dot(jnp.concatenate([high, low, high], 1), g_ref[...], preferred_element_type=F32)
            reals.append((z[:, :128] * cosine + z[:, 128:] * sine).astype(BF16))
            imags.append((z[:, 128:] * cosine - z[:, :128] * sine).astype(BF16))
        moved = jnp.dot(jnp.concatenate(reals + imags, 1), m_ref[...], preferred_element_type=F32).astype(BF16)
        for j in range(BANDS):
            for kh in range(4):
                obuf[j * 4 + kh] = moved[j * part : (j + 1) * part, kh * 128 : (kh + 1) * 128]

    def send(h, obuf):
        return pltpu.make_async_copy(obuf, out_hbm.at[:, pl.ds(h * part, part), :], tsems.at[2 + h])

    tables[0].wait()
    tables[1].wait()
    reorder(0, dbuf0)
    finish(0, dbuf0, obuf0)
    reorder(1, dbuf1)
    send(0, obuf0).start()
    finish(1, dbuf1, obuf1)
    send(1, obuf1).start()
    send(0, obuf0).wait()
    send(1, obuf1).wait()


def channelize(voltages, delays, phases, flags):
    vm = pl.BlockSpec(memory_space=pltpu.VMEM)
    hbm = pl.BlockSpec(memory_space=pl.ANY)
    limits = pltpu.CompilerParams(vmem_limit_bytes=LIMIT)

    block = pltpu.VMEM((2 * NFINE, STN, 128), F32)
    table = pltpu.VMEM((BANDS, STN, 128), F32)
    frames = pltpu.VMEM((STN, FRAMES * NFFT + RIM), BF16)
    rim, begun, weights, small = pl.pallas_call(
        first_kernel,
        out_shape=[
            pltpu.VMEM((STN, RIM), BF16),
            frames,
            pltpu.VMEM((1024, 256), BF16),
            pltpu.VMEM((3, 1, STN), jnp.int32),
        ],
        in_specs=[hbm] * 5,
        out_specs=[vm] * 4,
        scratch_shapes=[pltpu.SemaphoreType.DMA((7,))],
        compiler_params=limits,
        name="first",
    )(
        far(voltages),
        far(jnp.asarray(coarse_weights())),
        far(delays.reshape(1, STN)),
        far(phases.reshape(1, STN)),
        far(flags.reshape(1, STN)),
    )
    rim = lax.ppermute(rim, "tm", [(1, 0), (2, 1), (3, 2)])
    coarse, tcos, tsin, _ = pl.pallas_call(
        coarse_kernel,
        out_shape=[block, table, table, frames],
        in_specs=[hbm, vm, vm, vm],
        out_specs=[vm] * 4,
        scratch_shapes=[pltpu.SemaphoreType.DMA((6,))],
        input_output_aliases={1: 3},
        compiler_params=limits,
        name="coarse",
    )(far(voltages), near(begun), near(weights), near(small))
    half = (128, STN // 2, 128)
    return pl.pallas_call(
        fine_kernel,
        out_shape=jax.ShapeDtypeStruct((128, STN, 128), BF16),
        in_specs=[vm] * 5 + [hbm, hbm],
        out_specs=hbm,
        scratch_shapes=[
            pltpu.VMEM((768, 256), BF16),
            pltpu.VMEM((512, 512), BF16),
            pltpu.VMEM(half, F32),
            pltpu.VMEM(half, F32),
            pltpu.VMEM(half, BF16),
            pltpu.VMEM(half, BF16),
            pltpu.SemaphoreType.DMA((4,)),
        ],
        compiler_params=limits,
        name="fine",
    )(near(coarse), near(rim), near(weights), near(tcos), near(tsin), far(jnp.asarray(fine_weights())), far(jnp.asarray(send_moves())))


def correlate_kernel(r_ref, m_ref, out_hbm, x_buf, s_buf, o_buf, sems):
    sign = jnp.where(lax.broadcasted_iota(jnp.int32, (1024, 128), 1) < 64, 1.0, -1.0)

    def prepare(pair):
        parts = [r_ref[t * STN : (t + 1) * STN].reshape(1024, 128) for t in range(4)]
        both = jnp.dot(
            jnp.concatenate(parts, 1), m_ref[:, pair * 256 : (pair + 1) * 256], preferred_element_type=F32
        )
        for k in range(2):
            value = both[:, k * 128 : (k + 1) * 128]
            x_buf[pair * 2 + k] = value.astype(BF16)
            s_buf[pair * 2 + k] = (pltpu.roll(value, 64, 1) * sign).astype(BF16)

    def product(left, right):
        return lax.dot_general(left, right, (((1,), (1,)), ((), ())), preferred_element_type=F32)

    def send(g, j):
        cols = pl.ds(j * 256, 256)
        return pltpu.make_async_copy(o_buf.at[g, :, cols], out_hbm.at[g, :, cols], sems.at[g, j])

    row = lax.broadcasted_iota(jnp.int32, (256, 256), 0)
    upper = lax.broadcasted_iota(jnp.int32, (256, 256), 1) >= row
    prepare(0)
    for g in range(4):
        for j in range(4):
            low, high = j * 256, (j + 1) * 256
            column = x_buf[g, low:high, :]
            real = product(x_buf[g, :high, :], column)
            imag = product(s_buf[g, low:, :], column)
            if j > 0:
                o_buf[g, :low, low:high] = real[:low]
            if j < 3:
                o_buf[g, high:, low:high] = imag[256:]
            o_buf[g, low:high, low:high] = jnp.where(upper, real[low:], imag[:256])
            send(g, j).start()
        if g == 0:
            prepare(1)
    for g in range(4):
        for j in range(4):
            send(g, j).wait()


def correlate(received):
    return pl.pallas_call(
        correlate_kernel,
        out_shape=jax.ShapeDtypeStruct((4, 1024, 1024), F32),
        in_specs=[pl.BlockSpec(memory_space=pltpu.VMEM)] * 2,
        out_specs=pl.BlockSpec(memory_space=pl.ANY),
        scratch_shapes=[
            pltpu.VMEM((4, 1024, 128), BF16),
            pltpu.VMEM((4, 1024, 128), BF16),
            pltpu.VMEM((4, 1024, 1024), F32),
            pltpu.SemaphoreType.DMA((4, 4)),
        ],
        compiler_params=pltpu.CompilerParams(vmem_limit_bytes=LIMIT),
        name="correlate",
    )(near(received), near(jnp.asarray(group_moves())))


def local(voltages, delays, phases, flags):
    sent = channelize(voltages, delays, phases, flags)
    received = lax.all_to_all(sent, ("tm", "stn"), 0, 0, tiled=True)
    return correlate(received)


def solution(mesh):
    in_specs = (P("stn", "tm"), P("stn"), P("stn"), P("stn"))
    out_specs = P(("tm", "stn"), None, None)
    return jax.shard_map(local, mesh=mesh, in_specs=in_specs, out_specs=out_specs, check_vma=False)
```

```python
import math

import jax
import jax.numpy as jnp
import numpy as np
from jax import lax
from jax.experimental import pallas as pl
from jax.experimental.pallas import tpu as pltpu
from jax.sharding import PartitionSpec as P

NFFT = 512
TAPS = 4
NFINE = 64
AVG = 4
BANDS = 32
STN = 32
SPEC = 4
FRAMES = SPEC * NFINE
RIM = (TAPS - 1) * NFFT
CHUNK = 16
WIDE = 32
LIMIT = 40 * 2**20
TURN = NFFT * NFINE
F32 = jnp.float32
BF16 = jnp.bfloat16


def near(array):
    return pltpu.with_memory_space_constraint(array, pltpu.VMEM)


def far(array):
    return pltpu.with_memory_space_constraint(array, pltpu.HBM)


def split_two(table):
    high = table.astype(jnp.bfloat16)
    low = (table - high.astype(np.float64)).astype(jnp.bfloat16)
    return high, low


def coarse_weights():
    length = TAPS * NFFT
    places = np.arange(length, dtype=np.float64)
    offsets = (places - length / 2 + 0.5) / NFFT
    taper = 0.54 - 0.46 * np.cos(2.0 * math.pi * places / (length - 1))
    window = (np.sinc(offsets) * taper).reshape(TAPS, NFFT)
    product = (np.arange(NFFT)[:, None] * (np.arange(BANDS) + 1)[None, :]) % NFFT
    angles = product * (2.0 * math.pi / NFFT)
    table = np.concatenate([np.cos(angles), -np.sin(angles)], 1) / math.sqrt(NFFT)
    taps = [np.concatenate(split_two(window[t][:, None] * table), 1) for t in range(TAPS)]
    return np.block([[taps[0], taps[1]], [taps[2], taps[3]]])


def fine_weights():
    product = (np.arange(NFINE)[:, None] * (np.arange(NFINE) - NFINE // 2)[None, :]) % NFINE
    angles = product * (2.0 * math.pi / NFINE)
    cosine = np.cos(angles) / math.sqrt(NFINE)
    sine = np.sin(angles) / math.sqrt(NFINE)
    full = np.zeros((2, 2, NFINE, 2, NFINE, 2))
    pair = {(0, 0): cosine, (0, 1): -sine, (1, 0): sine, (1, 1): cosine}
    for (part_in, part_out), table in pair.items():
        for p in range(2):
            full[part_in, p, :, part_out, :, p] = table
    high, low = split_two(full.reshape(4 * NFINE, 4 * NFINE))
    return np.concatenate([high, high, low], 0)


def send_moves():
    source = np.arange(512).reshape(4, 4, 32).transpose(1, 0, 2).reshape(-1)
    return np.eye(512)[:, source].astype(jnp.bfloat16)


def group_moves():
    source = np.arange(512).reshape(4, 2, 2, 4, 8).transpose(3, 1, 2, 0, 4).reshape(-1)
    return np.eye(512)[:, source].astype(jnp.bfloat16)


def frames_copy(volt_hbm, xbuf, sem, start, count):
    where = pl.ds(start * NFFT, count * NFFT)
    return pltpu.make_async_copy(volt_hbm.at[:, where], xbuf.at[:, where], sem)


def first_kernel(volt_hbm, w_hbm, d_hbm, p_hbm, f_hbm, rim_ref, xbuf, w_ref, small, sems):
    copies = [pltpu.make_async_copy(volt_hbm.at[:, pl.ds(0, RIM)], rim_ref, sems.at[0])]
    for k, source in enumerate((d_hbm, p_hbm, f_hbm)):
        copies.append(pltpu.make_async_copy(source, small.at[k], sems.at[1 + k]))
    for k, start in enumerate((0, NFINE)):
        copies.append(frames_copy(volt_hbm, xbuf, sems.at[4 + k], start, WIDE + 3))
    copies.append(pltpu.make_async_copy(w_hbm, w_ref, sems.at[6]))
    for each in copies:
        each.start()
    xbuf[:, FRAMES * NFFT :] = jnp.zeros((STN, RIM), BF16)
    for each in copies:
        each.wait()


def coarse_kernel(volt_hbm, x_in, w_ref, small, cbuf, tcos, tsin, xbuf, sems):
    segments = ((35, 29), (99, 32), (131, 32), (192, 35), (163, 29), (227, 29))
    copies = [frames_copy(volt_hbm, xbuf, sems.at[k], *segment) for k, segment in enumerate(segments)]
    for each in copies:
        each.start()
    first_half = lax.broadcasted_iota(jnp.int32, (WIDE * STN, 128), 1) < 64
    diagonal = lax.broadcasted_iota(jnp.int32, (STN, STN), 0) == lax.broadcasted_iota(jnp.int32, (STN, STN), 1)

    def column(ref):
        spread = jnp.broadcast_to(ref[...].astype(F32), (STN, STN))
        picked = jnp.sum(jnp.where(diagonal, spread, 0.0), 1, keepdims=True)
        return jnp.broadcast_to(picked, (STN, 128))

    delay = column(small.at[0]).astype(jnp.int32)
    phase = column(small.at[1]).astype(jnp.int32)
    keep = column(small.at[2]) * 0.125
    fine_id = lax.broadcasted_iota(jnp.int32, (STN, 128), 1) // 2 - NFINE // 2

    def rotation(band):
        index = (delay * ((band + 1) * NFINE + fine_id) + phase) & (TURN - 1)
        quarter = (index + TURN // 8) >> 13
        angle = (index - (quarter << 13)).astype(F32) * (2.0 * math.pi / TURN)
        square = angle * angle
        sine = -1.9515295891e-4 * square + 8.3321608736e-3
        sine = (sine * square - 1.6666654611e-1) * square * angle + angle
        cosine = 2.443315711809948e-5 * square - 1.388731625493765e-3
        cosine = (cosine * square + 4.166664568298827e-2) * square * square - 0.5 * square + 1.0
        swap = (quarter & 1) == 1
        real = jnp.where(swap, sine, cosine) * keep
        imag = jnp.where(swap, cosine, sine) * keep
        real = jnp.where(((quarter + 1) & 2) == 2, -real, real)
        imag = jnp.where((quarter & 2) == 2, -imag, imag)
        tcos[band] = real
        tsin[band] = imag

    def spectrum(base):
        def frame(j):
            return xbuf[:, pl.ds(pl.multiple_of((base + j) * NFFT, NFFT), NFFT)]

        frames = [frame(j) for j in range(WIDE + 3)]
        left = jnp.concatenate(frames[: WIDE + 1], 0)
        right = jnp.concatenate(frames[2:], 0)
        both = jnp.concatenate([left, right], 1)
        z = jnp.dot(both, w_ref[...], preferred_element_type=F32)
        return z[: WIDE * STN, :128] + z[STN:, 128:]

    @pl.loop(0, 4)
    def _(i):
        part = i % 2
        a = (i // 2) * 8 + part * 2

        for k in range(3):

            @pl.when(i == k + 1)
            def _():
                copies[2 * k].wait()
                copies[2 * k + 1].wait()

        y0 = spectrum(a * CHUNK)
        y1 = spectrum((a + 4) * CHUNK)
        value = jnp.where(first_half, y0, y1) + pltpu.roll(jnp.where(first_half, y1, y0), 64, 1)
        cbuf[pl.ds(pl.multiple_of(i * WIDE, WIDE), WIDE)] = value.reshape(WIDE, STN, 128)
        for j in range(8):
            rotation(i * 8 + j)


def fine_kernel(
    c_ref, rim_ref, w_ref, tcos, tsin, g_hbm, m_hbm, out_hbm, g_ref, m_ref, dbuf0, dbuf1, obuf0, obuf1, tsems
):
    tables = [
        pltpu.make_async_copy(source, target, tsems.at[k])
        for k, (source, target) in enumerate(((g_hbm, g_ref), (m_hbm, m_ref)))
    ]
    tables[0].start()
    tables[1].start()
    none = jnp.zeros((STN, NFFT), BF16)
    rim = [rim_ref[:, k * NFFT : (k + 1) * NFFT] for k in range(TAPS - 1)]
    left = jnp.concatenate([none, none, none, rim[0]], 0)
    right = jnp.concatenate([none] + rim, 0)
    z = jnp.dot(jnp.concatenate([left, right], 1), w_ref[...], preferred_element_type=F32)
    y = z[: 3 * STN, :128] + z[STN:, 128:]
    second_half = lax.broadcasted_iota(jnp.int32, (3 * STN, 128), 1) >= 64
    extra = jnp.where(second_half, y + pltpu.roll(y, 64, 1), 0.0).reshape(3, STN, 128)
    last = 2 * NFINE - 3
    part = STN // 2
    rows = BANDS * part

    def reorder(h, dbuf):
        for sb in range(2):
            start = h * part + sb * 8
            ending = c_ref[last:, start : start + 8, :] + extra[:, start : start + 8, :]
            block = jnp.concatenate([c_ref[:last, start : start + 8, :], ending], 0)
            streams = jnp.swapaxes(block, 0, 1)
            turned = jnp.stack([streams[s].T for s in range(8)], 0)
            dbuf[:, sb * 8 : (sb + 1) * 8, :] = jnp.swapaxes(turned, 0, 1)

    def finish(h, dbuf, obuf):
        reals, imags = [], []
        cosine = tcos[:, h * part : (h + 1) * part, :].reshape(rows, 128)
        sine = tsin[:, h * part : (h + 1) * part, :].reshape(rows, 128)
        for p in range(2):
            starts = [(p * 2 + q) * BANDS for q in range(2)]
            data = jnp.concatenate([dbuf[x : x + BANDS].reshape(rows, 128) for x in starts], 1)
            high = data.astype(BF16)
            low = (data - high.astype(F32)).astype(BF16)
            z = jnp.dot(jnp.concatenate([high, low, high], 1), g_ref[...], preferred_element_type=F32)
            reals.append((z[:, :128] * cosine + z[:, 128:] * sine).astype(BF16))
            imags.append((z[:, 128:] * cosine - z[:, :128] * sine).astype(BF16))
        moved = jnp.dot(jnp.concatenate(reals + imags, 1), m_ref[...], preferred_element_type=F32).astype(BF16)
        for j in range(BANDS):
            for kh in range(4):
                obuf[j * 4 + kh] = moved[j * part : (j + 1) * part, kh * 128 : (kh + 1) * 128]

    def send(h, obuf):
        return pltpu.make_async_copy(obuf, out_hbm.at[:, pl.ds(h * part, part), :], tsems.at[2 + h])

    reorder(0, dbuf0)
    tables[0].wait()
    tables[1].wait()
    finish(0, dbuf0, obuf0)
    reorder(1, dbuf1)
    send(0, obuf0).start()
    finish(1, dbuf1, obuf1)
    send(1, obuf1).start()
    send(0, obuf0).wait()
    send(1, obuf1).wait()


def channelize(voltages, delays, phases, flags):
    vm = pl.BlockSpec(memory_space=pltpu.VMEM)
    hbm = pl.BlockSpec(memory_space=pl.ANY)
    limits = pltpu.CompilerParams(vmem_limit_bytes=LIMIT)

    block = pltpu.VMEM((2 * NFINE, STN, 128), F32)
    table = pltpu.VMEM((BANDS, STN, 128), F32)
    frames = pltpu.VMEM((STN, FRAMES * NFFT + RIM), BF16)
    rim, begun, weights, small = pl.pallas_call(
        first_kernel,
        out_shape=[
            pltpu.VMEM((STN, RIM), BF16),
            frames,
            pltpu.VMEM((1024, 256), BF16),
            pltpu.VMEM((3, 1, STN), jnp.int32),
        ],
        in_specs=[hbm] * 5,
        out_specs=[vm] * 4,
        scratch_shapes=[pltpu.SemaphoreType.DMA((7,))],
        compiler_params=limits,
        name="first",
    )(
        far(voltages),
        far(jnp.asarray(coarse_weights())),
        far(delays.reshape(1, STN)),
        far(phases.reshape(1, STN)),
        far(flags.reshape(1, STN)),
    )
    rim = lax.ppermute(rim, "tm", [(1, 0), (2, 1), (3, 2)])
    coarse, tcos, tsin, _ = pl.pallas_call(
        coarse_kernel,
        out_shape=[block, table, table, frames],
        in_specs=[hbm, vm, vm, vm],
        out_specs=[vm] * 4,
        scratch_shapes=[pltpu.SemaphoreType.DMA((6,))],
        input_output_aliases={1: 3},
        compiler_params=limits,
        name="coarse",
    )(far(voltages), near(begun), near(weights), near(small))
    half = (128, STN // 2, 128)
    return pl.pallas_call(
        fine_kernel,
        out_shape=jax.ShapeDtypeStruct((128, STN, 128), BF16),
        in_specs=[vm] * 5 + [hbm, hbm],
        out_specs=hbm,
        scratch_shapes=[
            pltpu.VMEM((768, 256), BF16),
            pltpu.VMEM((512, 512), BF16),
            pltpu.VMEM(half, F32),
            pltpu.VMEM(half, F32),
            pltpu.VMEM(half, BF16),
            pltpu.VMEM(half, BF16),
            pltpu.SemaphoreType.DMA((4,)),
        ],
        compiler_params=limits,
        name="fine",
    )(near(coarse), near(rim), near(weights), near(tcos), near(tsin), far(jnp.asarray(fine_weights())), far(jnp.asarray(send_moves())))


def correlate_kernel(r_ref, m_ref, out_hbm, x_buf, s_buf, o_buf, sems):
    sign = jnp.where(lax.broadcasted_iota(jnp.int32, (1024, 128), 1) < 64, 1.0, -1.0)

    def prepare(pair):
        parts = [r_ref[t * STN : (t + 1) * STN].reshape(1024, 128) for t in range(4)]
        both = jnp.dot(
            jnp.concatenate(parts, 1), m_ref[:, pair * 256 : (pair + 1) * 256], preferred_element_type=F32
        )
        for k in range(2):
            value = both[:, k * 128 : (k + 1) * 128]
            x_buf[pair * 2 + k] = value.astype(BF16)
            s_buf[pair * 2 + k] = (pltpu.roll(value, 64, 1) * sign).astype(BF16)

    def product(left, right):
        return lax.dot_general(left, right, (((1,), (1,)), ((), ())), preferred_element_type=F32)

    def send(g, j):
        cols = pl.ds(j * 256, 256)
        return pltpu.make_async_copy(o_buf.at[g, :, cols], out_hbm.at[g, :, cols], sems.at[g, j])

    row = lax.broadcasted_iota(jnp.int32, (256, 256), 0)
    upper = lax.broadcasted_iota(jnp.int32, (256, 256), 1) >= row
    prepare(0)
    prepare(1)
    for g in range(4):
        for j in range(4):
            low, high = j * 256, (j + 1) * 256
            column = x_buf[g, low:high, :]
            if j > 0:
                o_buf[g, :low, low:high] = product(x_buf[g, :low, :], column)
            if j < 3:
                o_buf[g, high:, low:high] = product(s_buf[g, high:, :], column)
            real = product(x_buf[g, low:high, :], column)
            imag = product(s_buf[g, low:high, :], column)
            o_buf[g, low:high, low:high] = jnp.where(upper, real, imag)
            send(g, j).start()
    for g in range(4):
        for j in range(4):
            send(g, j).wait()


def correlate(received):
    return pl.pallas_call(
        correlate_kernel,
        out_shape=jax.ShapeDtypeStruct((4, 1024, 1024), F32),
        in_specs=[pl.BlockSpec(memory_space=pltpu.VMEM)] * 2,
        out_specs=pl.BlockSpec(memory_space=pl.ANY),
        scratch_shapes=[
            pltpu.VMEM((4, 1024, 128), BF16),
            pltpu.VMEM((4, 1024, 128), BF16),
            pltpu.VMEM((4, 1024, 1024), F32),
            pltpu.SemaphoreType.DMA((4, 4)),
        ],
        compiler_params=pltpu.CompilerParams(vmem_limit_bytes=LIMIT),
        name="correlate",
    )(near(received), near(jnp.asarray(group_moves())))


def local(voltages, delays, phases, flags):
    sent = channelize(voltages, delays, phases, flags)
    received = lax.all_to_all(sent, ("tm", "stn"), 0, 0, tiled=True)
    return correlate(received)


def solution(mesh):
    in_specs = (P("stn", "tm"), P("stn"), P("stn"), P("stn"))
    out_specs = P(("tm", "stn"), None, None)
    return jax.shard_map(local, mesh=mesh, in_specs=in_specs, out_specs=out_specs, check_vma=False)
```
